32 devices in a mesh: real: 4 (over y, core), sky: 8 (over z, x).
Axes of the slice: x: 2, y: 2, z: 4, core: 2. Of those that a mesh axis runs over, the one named last changes fastest.
Arguments:
- potential_stock: bfloat16 [8, 256, 16384], P('real', 'sky'), may hold values from -6 to 6
- plane_pick: int32 [4], replicated, may hold values from 0 to 7, as said below
- col_shift: int32 [4, 4], P('real'), may hold values from 0 to 16383
- mirror: int32 [4, 4], P('real'), may hold values from 0 to 1
- subcell: int32 [32, 16], P('sky'), may hold values from 0 to 15
- lens_weight: float32 [4], replicated, may hold values from 0.02 to 0.08
Outputs:
- deflect: float32 [2, 4, 256, 2048], P(None, 'real', 'sky')
- distort: float32 [4, 4, 256, 2048], P(None, 'real', 'sky')
The draws below stay inside these ranges and needn't reach their ends.
Inputs may be any that keep to these rules, and one draw needn't show every extreme that they name: `plane_pick`: the 4 entries are distinct stored entries; entry q is held by the realization group q // 2.
All inputs are finite; a program needn't handle non-finite values.
Results may differ from the reference program's by a relative error of at most 0.0003.
Values may be sent and summed in bfloat16 or wider, within the bound.
A program may use at most 64 MiB of HBM per device.

```python
import math
import jax
import jax.numpy as jnp
from jax import lax

COLS = 2048
PLANE_COLS = 16384
PLANES = 4
SUB = 4
TILE_R = 8
TILE_C = 128
WIN_ROWS = 256
STOCK = 8
N_REAL = 4


def draw_plane_pick(key, part):
    first_key = jax.random.fold_in(key, 11)
    second_key = jax.random.fold_in(key, 23)
    middle = jax.random.permutation(first_key, STOCK - 2)[:PLANES - 2] + 1
    chosen = jnp.concatenate([jnp.array([0, STOCK - 1], jnp.int32), middle.astype(jnp.int32)])
    order = jax.random.permutation(second_key, PLANES)
    return chosen[order].astype(jnp.int32)


def touch_ends(values, rng, low, largest):
    shape = values.shape
    place = [jax.random.randint(jax.random.fold_in(rng, axis), (), 0, shape[axis]) for axis in range(len(shape))]
    values = values.at[tuple(place)].set(low)
    longest = shape.index(max(shape))
    place[longest] = (place[longest] + 1) % shape[longest]
    return values.at[tuple(place)].set(largest)


def block_levels(stream_key, shape, split, least, largest):
    gain = 1.0
    for position, blocks in split:
        draws = jax.random.uniform(jax.random.fold_in(jax.random.fold_in(stream_key, 6), position), (blocks,), jnp.float32, least / len(split), largest / len(split))
        gain = gain * jnp.repeat(jnp.exp(draws), shape[position] // blocks).reshape((-1,) + (1,) * (len(shape) - 1 - position))
    return gain


def scatter_about(rng, extent, spread, reach, split=(), held_as=jnp.bfloat16):
    factor_of = block_levels(rng, extent, split, -0.22, 0.18) if split else 1.0
    values = jax.random.normal(rng, extent, jnp.float32) * spread * factor_of
    return jnp.minimum(jnp.maximum(values, -reach), reach).astype(held_as)


def setup_inputs(seed: int = 0) -> dict:
    key_list = jax.random.split(jax.random.key(seed), 7)
    return {
        "potential_stock": scatter_about(key_list[0], (STOCK, WIN_ROWS, PLANE_COLS), 1.0, 6.0, ((0, 4), (1, 8))),
        "plane_pick": draw_plane_pick(jax.random.fold_in(key_list[6], 71), 0),
        "col_shift": touch_ends(jax.random.randint(key_list[2], (N_REAL, PLANES), 0, PLANE_COLS), jax.random.fold_in(key_list[2], 1), 0, PLANE_COLS - 1).astype(jnp.int32),
        "mirror": touch_ends(jax.random.randint(key_list[3], (N_REAL, PLANES), 0, 2), jax.random.fold_in(key_list[3], 1), 0, 1).astype(jnp.int32),
        "subcell": touch_ends(jax.random.randint(key_list[4], (WIN_ROWS // TILE_R, COLS // TILE_C), 0, SUB * SUB), jax.random.fold_in(key_list[4], 1), 0, (SUB * SUB) - 1).astype(jnp.int32),
        "lens_weight": jnp.clip(jnp.exp(jax.random.uniform(key_list[5], (PLANES,), jnp.float32, math.log(0.02), math.log(0.08))), 0.02, 0.08),
    }


first_coef = (1.0 / 12.0, -8.0 / 12.0, 0.0, 8.0 / 12.0, -1.0 / 12.0)
second_coef = (-1.0 / 12.0, 16.0 / 12.0, -30.0 / 12.0, 16.0 / 12.0, -1.0 / 12.0)


def cubic_weights(frac):
    sq = frac * frac
    cube = sq * frac
    return ((-cube + 2.0 * sq - frac) * 0.5, (3.0 * cube - 5.0 * sq + 2.0) * 0.5,
            (-3.0 * cube + 4.0 * sq + frac) * 0.5, (cube - sq) * 0.5)


def tap_weights(subcell):
    frac_x = ((subcell % SUB).astype(jnp.float32) + 0.5) / SUB
    frac_y = ((subcell // SUB).astype(jnp.float32) + 0.5) / SUB
    weights_x = tuple(w[:, None, :, None] for w in cubic_weights(frac_x))
    weights_y = tuple(w[:, None, :, None] for w in cubic_weights(frac_y))
    return weights_x, weights_y


def derivatives(tile):
    nrows = tile.shape[0] - 5
    ncols = tile.shape[1] - 5

    def window(drow, dcol):
        return tile[3 + drow:3 + drow + nrows, 3 + dcol:3 + dcol + ncols]

    grad_x = sum(first_coef[q] * window(0, q - 2) for q in range(5) if q != 2)
    grad_y = sum(first_coef[q] * window(q - 2, 0) for q in range(5) if q != 2)
    hess_xx = sum(second_coef[q] * window(0, q - 2) for q in range(5))
    hess_yy = sum(second_coef[q] * window(q - 2, 0) for q in range(5))
    hess_xy = sum(first_coef[p] * first_coef[q] * window(p - 2, q - 2)
                  for p in range(5) for q in range(5) if p != 2 and q != 2)
    return grad_x, grad_y, hess_xx, hess_yy, hess_xy


def sample(field, weights_x, weights_y, nrows, ncols):
    total = jnp.zeros((nrows // TILE_R, TILE_R, ncols // TILE_C, TILE_C), jnp.float32)
    for brow in range(4):
        inner = jnp.zeros_like(total)
        for acol in range(4):
            piece = field[brow:brow + nrows, acol:acol + ncols]
            piece = piece.reshape(nrows // TILE_R, TILE_R, ncols // TILE_C, TILE_C)
            inner = inner + weights_x[acol] * piece
        total = total + weights_y[brow] * inner
    return total.reshape(nrows, ncols)


def advance(state, tile, weights_x, weights_y, lens):
    nrows = tile.shape[0] - 8
    ncols = tile.shape[1] - 8
    fields = derivatives(tile.astype(jnp.float32))
    grad_x, grad_y, hess_xx, hess_yy, hess_xy = [sample(f, weights_x, weights_y, nrows, ncols) for f in fields]
    shift_x, shift_y, a_11, a_12, a_21, a_22 = state
    shift_x = shift_x + lens * grad_x
    shift_y = shift_y + lens * grad_y
    new_11 = a_11 - lens * (hess_xx * a_11 + hess_xy * a_21)
    new_12 = a_12 - lens * (hess_xx * a_12 + hess_xy * a_22)
    new_21 = a_21 - lens * (hess_xy * a_11 + hess_yy * a_21)
    new_22 = a_22 - lens * (hess_xy * a_12 + hess_yy * a_22)
    return (shift_x, shift_y, new_11, new_12, new_21, new_22)


def reference(potential_stock, plane_pick, col_shift, mirror, subcell, lens_weight):
    weights_x, weights_y = tap_weights(subcell)
    offsets = jnp.arange(-4, COLS + 4, dtype=jnp.int32)

    def trace_one(pair):
        shift_row, mirror_row = pair
        zeros = jnp.zeros((WIN_ROWS, COLS), jnp.float32)
        ones = jnp.ones((WIN_ROWS, COLS), jnp.float32)
        state = (zeros, zeros, ones, zeros, zeros, ones)
        for plane in range(PLANES):
            band = potential_stock[plane_pick[plane]]
            flipped = jnp.where(mirror_row[plane] == 1, band[:, ::-1], band)
            columns = ((shift_row[plane] + offsets) % PLANE_COLS).astype(jnp.int32)
            view = jnp.take(flipped, columns, axis=1)
            view = jnp.concatenate([view[-4:], view, view[:4]], axis=0)
            state = advance(state, view, weights_x, weights_y, lens_weight[plane])
        return state

    result = lax.map(trace_one, (col_shift, mirror))
    deflect = jnp.stack([result[0], result[1]])
    distort = jnp.stack([result[2], result[3], result[4], result[5]])
    return deflect, distort
```

```python
import functools

import jax
import jax.numpy as jnp
import numpy as np
from jax import lax
from jax.experimental import pallas as pl
from jax.experimental.pallas import tpu as pltpu
from jax.sharding import PartitionSpec as P

SUB = 4
TILE_R = 8
TILE_C = 128
EDGE = 4
MESH = pl.DeviceIdType.MESH

first_coef = (1.0 / 12.0, -8.0 / 12.0, 0.0, 8.0 / 12.0, -1.0 / 12.0)
second_coef = (-1.0 / 12.0, 16.0 / 12.0, -30.0 / 12.0, 16.0 / 12.0, -1.0 / 12.0)


def cubic(t):
    return (
        (-(t**3) + 2 * t**2 - t) / 2,
        (3 * t**3 - 5 * t**2 + 2) / 2,
        (-3 * t**3 + 4 * t**2 + t) / 2,
        (t**3 - t**2) / 2,
    )


def convolved(taps, coef):
    out = [0.0] * 8
    for a, w in enumerate(taps):
        for q, c in enumerate(coef):
            out[a + q] += w * c
    return out


def filter_table():
    rows = []
    for o in range(SUB):
        taps = cubic((o + 0.5) / SUB)
        rows.append(list(taps) + convolved(taps, first_coef) + convolved(taps, second_coef))
    return rows


TABLE = filter_table()
NTAB = 20
X_SCALE = 12288.0


def column_filters():
    full = np.zeros((2 * TILE_C, SUB, 3, TILE_C))
    out = np.arange(TILE_C)
    for o, row in enumerate(TABLE):
        for m in range(4):
            full[out + 3 + m, o, 0, out] = row[m] * X_SCALE
        for m in range(8):
            full[out + 1 + m, o, 1, out] = row[4 + m] * X_SCALE
            full[out + 1 + m, o, 2, out] = row[12 + m] * X_SCALE
    full = np.rint(full.reshape(2 * TILE_C, SUB * 3 * TILE_C)).astype(np.float32)
    high = full.astype(jnp.bfloat16)
    low = (full - high.astype(np.float32)).astype(jnp.bfloat16)
    return np.concatenate([high, low], axis=0)


def each(count, fn):
    if count == 1:
        fn(0)
    else:
        lax.fori_loop(0, count, lambda n, carry: (fn(n), carry)[1], 0)


def total(flags):
    return sum(jnp.where(flag, 1, 0) for flag in flags)


def last_hit(hits, values):
    found = jnp.int32(0)
    for hit, value in zip(hits, values):
        found = jnp.where(hit, value, found)
    return found


def trace_kernel(
    slots,
    stock_ref, pick_ref, shift_ref, mirror_ref, subcell_ref, lens_ref, filt_ref,
    deflect_ref, distort_ref,
    stock_t, bank, stage, own, beside, beside_out, far, far_out,
    mine, metas, edge32, edge_out, before, after, flank32, pairs, filt_v,
    field_a, field_b, hess, table,
    local_sem, meta_send, meta_recv, push_send, push_recv, beside_send, beside_recv,
    far_send, far_recv, edge_send, edge_recv,
):
    held, blocks, ntiles = stock_ref.shape[:3]
    half = blocks // 2
    nrows, ncols = deflect_ref.shape[2:]
    cols = ntiles * TILE_C
    tiles = ncols // TILE_C
    planes = pick_ref.shape[0]
    peers, strips = lax.axis_size("real"), lax.axis_size("sky")
    chips = peers // 2
    me, strip = lax.axis_index("real"), lax.axis_index("sky")
    core, chip = lax.rem(me, 2), lax.div(me, 2)
    partner = me + 1 - 2 * core
    above = lax.rem(strip + strips - 1, strips)
    below = lax.rem(strip + 1, strips)
    outer = tiles * TILE_R
    head = outer + half * TILE_R
    span = field_a.shape[1]
    bf = jnp.bfloat16
    f32 = jnp.float32
    low = max(0, planes - (chips - 1) * slots)
    high = min(slots, planes)

    def block_of(side, i):
        return side * (blocks - 1) + (1 - 2 * side) * i

    def remote(src, dst, send_sem, recv_sem, r, s):
        return pltpu.make_async_remote_copy(
            src_ref=src, dst_ref=dst, send_sem=send_sem, recv_sem=recv_sem,
            device_id=(r, s), device_id_type=MESH)

    stock_copy = pltpu.make_async_copy(stock_ref, stock_t, local_sem.at[0])
    stock_copy.start()
    barrier = pltpu.get_barrier_semaphore()
    for off in range(1, peers):
        pl.semaphore_signal(
            barrier, inc=1, device_id=(lax.rem(me + off, peers), strip), device_id_type=MESH)
    for s in (above, below):
        pl.semaphore_signal(barrier, inc=1, device_id=(me, s), device_id_type=MESH)
    bank_copies = [
        pltpu.make_async_copy(
            stock_ref.at[:, block_of(core, i)], bank.at[core, :, i], local_sem.at[1 + i])
        for i in range(half)
    ]
    filt_copy = pltpu.make_async_copy(filt_ref, filt_v, local_sem.at[1 + half])
    for copy in bank_copies + [filt_copy]:
        copy.start()

    for k in range(mine.shape[1]):
        mine[0, k] = 2 * shift_ref[0, k] + mirror_ref[0, k] if k < planes else 0
    for o in range(SUB):
        for m in range(NTAB):
            table[o, m] = f32(TABLE[o][m] / X_SCALE)
    edge32[...] = jnp.zeros_like(edge32)
    stage[...] = jnp.zeros_like(stage)

    pick = [pick_ref[k] for k in range(planes)]
    group = [lax.div(q, held) for q in pick]
    entry = [lax.rem(q, held) for q in pick]
    away = [lax.rem(lax.div(g, 2) - chip + chips, chips) for g in group]
    lane = [lax.rem(g, 2) for g in group]
    turn = [jnp.where(away[k] == 0, jnp.where(group[k] == me, 0, 1), lane[k]) for k in range(planes)]
    key = [(away[k] * 2 + turn[k]) * held + entry[k] for k in range(planes)]
    order = [total([key[n] < key[k] for n in range(planes)]) for k in range(planes)]
    plane_at = [last_hit([n == v for n in order], range(planes)) for v in range(planes)]
    n_own = total([group[k] == me for k in range(planes)])
    n_chip = total([away[k] == 0 for k in range(planes)])
    n_away = [total([away[k] == off for k in range(planes)]) for off in range(chips)]

    def chosen(inside, j):
        rank = [total([inside[n] & (pick[n] < pick[k]) for n in range(planes)]) for k in range(planes)]
        hits = [inside[k] & (rank[k] == j) for k in range(planes)]
        return [last_hit(hits, value) for value in (range(planes), lane, entry)]

    own_pick = [chosen([g == me for g in group], j) for j in range(held)]
    chip_pick = [chosen([a == 0 for a in away], j) for j in range(slots)]

    lane_in = lax.broadcasted_iota(jnp.int32, (2 * TILE_C, TILE_C), 0)
    lane_out = lax.broadcasted_iota(jnp.int32, (2 * TILE_C, TILE_C), 1)

    def cut(read, code, sides, out):
        turned = lax.rem(code, 2)
        shift = lax.div(code, 2)
        step = 1 - 2 * turned
        start = turned * (cols + EDGE - 1 - shift) + (1 - turned) * (shift + cols - EDGE)
        start = lax.rem(start, cols)
        base = lax.div(start, TILE_C)
        inner = start - base * TILE_C
        each_rows = (tiles + 2) * TILE_R
        for u in range(tiles + 2):
            at = lax.rem(base + step * u + ntiles, ntiles)
            for i in range(sides * half):
                row = i * each_rows + u * TILE_R
                stage[row:row + TILE_R, :] = read(i, at)
        near = lane_in == inner + step * lane_out
        far_ = lane_in - TILE_C == inner + step * (lane_out - TILE_C)
        choose = (near & (lane_in < TILE_C)) | (far_ & (lane_in >= TILE_C))
        choose = choose.astype(f32).astype(bf)
        n = sides * half * each_rows
        view = jnp.dot(
            jnp.concatenate([stage[0:n, :], stage[TILE_R:n + TILE_R, :]], axis=1), choose,
            preferred_element_type=f32)
        for x in range(sides):
            at = [(x * half + i) * each_rows for i in range(half)]
            rest = [view[a + outer:a + outer + TILE_R] for a in at]
            body_rows = [view[a:a + outer] for a in at]
            whole = jnp.concatenate(body_rows[:1] + rest + body_rows[1:], axis=0).astype(bf)
            out(x, whole)

    def code_of(r, k):
        return metas[r, 0, k]

    def own_read(e):
        def read(i, at):
            side, n = i // half, i % half
            return stock_t[e, block_of(side, n), at]
        return read

    def bank_read(c, e):
        def read(i, at):
            return bank[c, e, i, at]
        return read

    pl.semaphore_wait(barrier, peers + 1)

    def meta_copy(off):
        return remote(mine, metas.at[me], meta_send.at[off], meta_recv.at[off],
                      lax.rem(me + off, peers), strip)

    for off in range(1, peers):
        meta_copy(off).start()
    stock_copy.wait()
    push = [
        remote(stock_t.at[:, block_of(1 - core, i)], bank.at[core, :, i],
               push_send.at[i], push_recv.at[i], partner, strip)
        for i in range(half)
    ]
    for copy in push:
        copy.start()

    def keep(ref, *at):
        def out(x, whole):
            ref[(*at, x)] = whole
        return out

    for j in range(held):
        k, _, e = own_pick[j]
        cut(own_read(e), mine[0, k], 2, keep(own, j))

    for off in range(1, peers):
        meta_copy(off).wait()
    for copy in bank_copies:
        copy.wait()
    for copy in push:
        copy.wait()

    parts = (slice(0, head), slice(head, head + (half - 1) * outer))

    def far_copy(q, n, a, j):
        to = lax.rem(chip + n + 1, chips)
        return remote(
            far_out.at[n, a, j, parts[q]], far.at[chips - 2 - n, j, core, parts[q]],
            far_send.at[q, n, a, j], far_recv.at[q, chips - 2 - n, j, core],
            2 * to + a, strip)

    def far_arrived(q, n, j, side):
        return remote(
            far_out.at[n, 0, j, parts[q]], far.at[n, j, side, parts[q]],
            far_send.at[q, n, 0, j], far_recv.at[q, n, j, side], 2 * lax.rem(chip + n + 1, chips), strip)

    def send_far(q, j):
        def go(n):
            for a in range(2):
                far_copy(q, n, a, j).start()
        each(chips - 1, go)

    for j in range(slots):
        k, c, e = chip_pick[j]

        def make(n):
            to = lax.rem(chip + n + 1, chips)
            for a in range(2):
                def out(x, whole):
                    far_out[n, a, j] = whole
                cut(bank_read(c, e), code_of(2 * to + a, k), 1, out)
                far_copy(0, n, a, j).start()
        each(chips - 1, make)
        if j:
            send_far(1, j - 1)
    send_far(1, slots - 1)

    def beside_copy(j):
        return remote(beside_out.at[j], beside.at[j], beside_send.at[j], beside_recv.at[j], partner, strip)

    for j in range(held):
        k, _, e = own_pick[j]
        cut(own_read(e), code_of(partner, k), 2, keep(beside_out, j))
        beside_copy(j).start()

    def far_slots(v):
        if chips == 2:
            return [v - p for p in range(low, high + 1) if 0 <= v - p < slots]
        return list(range(min(v - low, slots - 1) + 1)) if v >= low else []

    arrived = set()

    def arrive(q, v):
        if v < high and "beside" not in arrived:
            arrived.add("beside")
            for j in range(held):
                beside_copy(j).wait_recv()
        for j in far_slots(v):
            if (q, j) not in arrived:
                arrived.add((q, j))

                def go(n):
                    for side in range(2):
                        far_arrived(q, n, j, side).wait_recv()
                each(chips - 1, go)

    def sources(v):
        found = []
        if v < high:
            if v < held:
                found.append((own.at[v], v < n_own))
            found += [(beside.at[j], (v - n_own == j) & (v < n_chip)) for j in range(held) if j <= v]
        gone = n_chip
        for n in range(chips - 1):
            for j in far_slots(v):
                found.append((far.at[n, j], (v - gone == j) & (j < n_away[n + 1])))
            gone = gone + n_away[n + 1]
        return found

    def selected(v, side, rows):
        got = None
        for ref, hit in sources(v):
            value = ref[side, rows, :]
            got = value if got is None else jnp.where(hit, value, got)
        return got

    def edge_copies(v):
        return [
            remote(edge_out.at[v, 0], after.at[v], edge_send.at[0, v], edge_recv.at[0, v], me, above),
            remote(edge_out.at[v, 1], before.at[v], edge_send.at[1, v], edge_recv.at[1, v], me, below),
        ]

    def lay(v, seg, side, first):
        left, right = slice(0, TILE_C), slice(TILE_C, 2 * TILE_C)
        pairs[v, seg, :, left] = selected(v, side, slice(first, first + outer))
        pairs[v, seg, 0:outer - TILE_R, right] = selected(v, side, slice(first + TILE_R, first + outer))

    def form_outer(v):
        arrive(0, v)
        for side in range(2):
            lay(v, side * half, side, 0)
            rest = selected(v, side, slice(outer, head))
            for i in range(half):
                pairs[v, side * half + i, outer - TILE_R:outer, TILE_C:2 * TILE_C] = (
                    rest[i * TILE_R:(i + 1) * TILE_R])
            shown = pairs[v, side * half, :, 0:TILE_C].astype(f32)
            ends = rest.astype(f32)[0:TILE_R]
            skip = side * (TILE_R - EDGE)
            for t in range(tiles):
                edge32[side, t * EDGE:(t + 1) * EDGE, :] = (
                    shown[t * TILE_R + skip:t * TILE_R + skip + EDGE])
            edge32[side, tiles * EDGE:(tiles + 1) * EDGE, :] = ends[skip:skip + EDGE]
            edge_out[v, side] = edge32[side].astype(bf)
        for copy in edge_copies(v):
            copy.start()

    def form_inner(v):
        arrive(1, v)
        for side in range(2):
            for i in range(1, half):
                lay(v, side * half + i, side, head + (i - 1) * outer)

    fields = (field_a, field_b)
    npairs = filt_ref.shape[1] // (2 * TILE_C)

    def process(v):
        for copy in edge_copies(v):
            copy.wait_recv()
        up = before[v].astype(f32)
        down = after[v].astype(f32)
        for t in range(tiles + 1):
            flank32[t, EDGE:2 * EDGE, :] = up[t * EDGE:(t + 1) * EDGE]
            flank32[t, 0:EDGE, :] = down[t * EDGE:(t + 1) * EDGE]
        for side in range(2):
            pairs[v, blocks, :, side * TILE_C:(side + 1) * TILE_C] = (
                flank32[side:tiles + side].reshape(outer, TILE_C).astype(bf))
        lens = lens_ref[plane_at[v]]

        def filter_pair(g, c):
            field = fields[g % 2]
            rows = slice(g * span * TILE_R, (g + 1) * span * TILE_R)
            lhs = jnp.concatenate([pairs[v, seg, rows, :] for seg in range(blocks + 1)], axis=0)
            got = jnp.dot(
                jnp.concatenate([lhs, lhs], axis=1), filt_v[:, 2 * c * TILE_C:2 * (c + 1) * TILE_C],
                preferred_element_type=f32)
            for h in range(2):
                part = got[:, h * TILE_C:(h + 1) * TILE_C].reshape(blocks + 1, span, TILE_R, TILE_C)
                for side in range(2):
                    for i in range(half):
                        first = TILE_R * (1 + (blocks - 1 - i if side else i))
                        field[2 * c + h, :, first:first + TILE_R, :] = part[side * half + i]
                field[2 * c + h, :, 0:TILE_R, :] = part[blocks]
                field[2 * c + h, :, TILE_R + nrows:2 * TILE_R + nrows, :] = part[blocks]

        def tile(i, j):
            field, jj = fields[(j // span) % 2], j % span
            o = subcell_ref[i, j]
            oy = o // SUB
            fx = (o - oy * SUB) * 3
            wy = [table[oy, m] for m in range(NTAB)]
            y0, y1, y2 = wy[:4], wy[4:12], wy[12:20]

            def row(q, n):
                return field[fx + q, jj, pl.ds(TILE_R + i * TILE_R + n, TILE_R), :]
            plain = [row(0, n) for n in range(-3, 5)]
            slope = [row(1, n) for n in range(-3, 5)]
            curve = [row(2, n) for n in range(-1, 3)]
            gx = sum(y0[b] * slope[b + 2] for b in range(4))
            xx = sum(y0[b] * curve[b] for b in range(4))
            xy = sum(y1[b] * slope[b] for b in range(8))
            gy = sum(y1[b] * plain[b] for b in range(8))
            yy = sum(y2[b] * plain[b] for b in range(8))
            at = slice(j * TILE_C, (j + 1) * TILE_C)
            rs = slice(i * TILE_R, (i + 1) * TILE_R)
            for n, grad in enumerate((gx, gy)):
                old = deflect_ref[n, 0, rs, at] if v else 0.0
                deflect_ref[n, 0, rs, at] = old + lens * grad
            for n, h in enumerate((xx, xy, yy)):
                hess[v, n, j, rs, :] = lens * h

        groups = tiles // span
        for c in range(npairs):
            filter_pair(0, c)
        for g in range(groups):
            todo = [(i, g * span + jj) for jj in range(span) for i in range(nrows // TILE_R)]
            count = -(-len(todo) // npairs)
            for c in range(npairs):
                if g + 1 < groups:
                    filter_pair(g + 1, c)
                for i, j in todo[c * count:(c + 1) * count]:
                    tile(i, j)

    filt_copy.wait()
    form_outer(0)
    form_outer(1)
    form_inner(0)
    for v in range(planes):
        process(v)
        if v + 2 < planes:
            form_outer(v + 2)
        if v + 1 < planes:
            form_inner(v + 1)

    shape = (TILE_R, TILE_C)
    for j in range(tiles):
        for i in range(nrows // TILE_R):
            rs = slice(i * TILE_R, (i + 1) * TILE_R)
            at = slice(j * TILE_C, (j + 1) * TILE_C)
            zero, one = jnp.zeros(shape, f32), jnp.ones(shape, f32)
            a11, a12, a21, a22 = one, zero, zero, one
            for k in range(planes):
                xx, xy, yy = [hess[order[k], n, j, rs, :] for n in range(3)]
                a11, a12, a21, a22 = (
                    a11 - (xx * a11 + xy * a21),
                    a12 - (xx * a12 + xy * a22),
                    a21 - (xy * a11 + yy * a21),
                    a22 - (xy * a12 + yy * a22),
                )
            for n, a in enumerate((a11, a12, a21, a22)):
                distort_ref[n, 0, rs, at] = a

    for j in range(held):
        beside_copy(j).wait_send()
    for j in range(slots):
        def done(n):
            for a in range(2):
                for q in range(2):
                    far_copy(q, n, a, j).wait_send()
        each(chips - 1, done)
    for v in range(planes):
        for copy in edge_copies(v):
            copy.wait_send()


def body(potential_stock, plane_pick, col_shift, mirror, subcell, lens_weight):
    held, rows, cols = potential_stock.shape
    peers = lax.axis_size("real")
    planes = plane_pick.shape[0]
    ncols = subcell.shape[1] * TILE_C
    nrows = subcell.shape[0] * TILE_R
    tiles = ncols // TILE_C
    blocks, half = rows // TILE_R, rows // (2 * TILE_R)
    chips = peers // 2
    ntiles = cols // TILE_C
    stock = potential_stock.reshape(held, blocks, TILE_R, ntiles, TILE_C).transpose(0, 1, 3, 2, 4)
    slots = min(planes, 2 * held)
    vm = pl.BlockSpec(memory_space=pltpu.VMEM)
    sm = pl.BlockSpec(memory_space=pltpu.SMEM)
    anyw = pl.BlockSpec(memory_space=pl.ANY)
    bf, f32 = jnp.bfloat16, jnp.float32
    dma = pltpu.SemaphoreType.DMA
    win = half * TILE_R * (tiles + 1)
    erows = -(-((tiles + 1) * EDGE) // 16) * 16
    srows = 2 * half * (tiles + 2) * TILE_R + 16
    span = next(d for d in (8, 4, 2, 1) if tiles % d == 0)
    filt = jnp.asarray(column_filters())
    meta = max(8, planes)
    return pl.pallas_call(
        functools.partial(trace_kernel, slots),
        out_shape=(
            pltpu.VMEM((2, 1, nrows, ncols), f32),
            pltpu.VMEM((4, 1, nrows, ncols), f32),
        ),
        in_specs=[anyw, sm, sm, sm, sm, sm, anyw],
        out_specs=(vm, vm),
        scratch_shapes=[
            pltpu.VMEM(stock.shape, bf),
            pltpu.VMEM((2, held, half, ntiles, TILE_R, TILE_C), bf),
            pltpu.VMEM((srows, TILE_C), bf),
            pltpu.VMEM((held, 2, win, TILE_C), bf),
            pltpu.VMEM((held, 2, win, TILE_C), bf),
            pltpu.VMEM((held, 2, win, TILE_C), bf),
            pltpu.VMEM((chips - 1, slots, 2, win, TILE_C), bf),
            pltpu.VMEM((chips - 1, 2, slots, win, TILE_C), bf),
            pltpu.SMEM((1, meta), jnp.int32),
            pltpu.SMEM((peers, 1, meta), jnp.int32),
            pltpu.VMEM((2, erows, TILE_C), f32),
            pltpu.VMEM((planes, 2, erows, TILE_C), bf),
            pltpu.VMEM((planes, erows, TILE_C), bf),
            pltpu.VMEM((planes, erows, TILE_C), bf),
            pltpu.VMEM((tiles + 1, TILE_R, TILE_C), f32),
            pltpu.VMEM((planes, blocks + 1, tiles * TILE_R, 2 * TILE_C), bf),
            pltpu.VMEM(filt.shape, bf),
            pltpu.VMEM((SUB * 3, span, nrows + 2 * TILE_R, TILE_C), f32),
            pltpu.VMEM((SUB * 3, span, nrows + 2 * TILE_R, TILE_C), f32),
            pltpu.VMEM((planes, 3, tiles, nrows, TILE_C), f32),
            pltpu.SMEM((SUB, NTAB), f32),
            dma((2 + half,)),
            dma((peers,)), dma((peers,)),
            dma((half,)), dma((half,)),
            dma((held,)), dma((held,)),
            dma((2, chips - 1, 2, slots)), dma((2, chips - 1, slots, 2)),
            dma((2, planes)), dma((2, planes)),
        ],
        compiler_params=pltpu.CompilerParams(
            collective_id=0, has_side_effects=True, vmem_limit_bytes=61 * 1024 * 1024),
        name="trace",
    )(stock, plane_pick, col_shift, mirror, subcell, lens_weight, filt)


def solution(mesh):
    return jax.shard_map(
        body,
        mesh=mesh,
        in_specs=(
            P("real", "sky", None),
            P(),
            P("real", None),
            P("real", None),
            P("sky", None),
            P(),
        ),
        out_specs=(P(None, "real", "sky", None), P(None, "real", "sky", None)),
        check_vma=False,
    )
```

```python
import functools

import jax
import jax.numpy as jnp
import numpy as np
from jax import lax
from jax.experimental import pallas as pl
from jax.experimental.pallas import tpu as pltpu
from jax.sharding import PartitionSpec as P

SUB = 4
TILE_R = 8
TILE_C = 128
EDGE = 4
MESH = pl.DeviceIdType.MESH

first_coef = (1.0 / 12.0, -8.0 / 12.0, 0.0, 8.0 / 12.0, -1.0 / 12.0)
second_coef = (-1.0 / 12.0, 16.0 / 12.0, -30.0 / 12.0, 16.0 / 12.0, -1.0 / 12.0)


def cubic(t):
    return (
        (-(t**3) + 2 * t**2 - t) / 2,
        (3 * t**3 - 5 * t**2 + 2) / 2,
        (-3 * t**3 + 4 * t**2 + t) / 2,
        (t**3 - t**2) / 2,
    )


def convolved(taps, coef):
    out = [0.0] * 8
    for a, w in enumerate(taps):
        for q, c in enumerate(coef):
            out[a + q] += w * c
    return out


def filter_table():
    rows = []
    for o in range(SUB):
        taps = cubic((o + 0.5) / SUB)
        rows.append(list(taps) + convolved(taps, first_coef) + convolved(taps, second_coef))
    return rows


TABLE = filter_table()
NTAB = 20
X_SCALE = 12288.0


def column_filters():
    full = np.zeros((2 * TILE_C, SUB, 3, TILE_C))
    out = np.arange(TILE_C)
    for o, row in enumerate(TABLE):
        for m in range(4):
            full[out + 3 + m, o, 0, out] = row[m] * X_SCALE
        for m in range(8):
            full[out + 1 + m, o, 1, out] = row[4 + m] * X_SCALE
            full[out + 1 + m, o, 2, out] = row[12 + m] * X_SCALE
    full = np.rint(full.reshape(2 * TILE_C, SUB * 3 * TILE_C)).astype(np.float32)
    high = full.astype(jnp.bfloat16)
    low = (full - high.astype(np.float32)).astype(jnp.bfloat16)
    return np.concatenate([high, low], axis=0)


def each(count, fn):
    if count == 1:
        fn(0)
    else:
        lax.fori_loop(0, count, lambda n, carry: (fn(n), carry)[1], 0)


def total(flags):
    return sum(jnp.where(flag, 1, 0) for flag in flags)


def last_hit(hits, values):
    found = jnp.int32(0)
    for hit, value in zip(hits, values):
        found = jnp.where(hit, value, found)
    return found


def level_kernel(per_chip, levels, pick_ref, level_ref):
    planes = pick_ref.shape[0]
    chip = [lax.div(pick_ref[k], per_chip) for k in range(planes)]
    most = jnp.int32(0)
    for k in range(planes):
        most = jnp.maximum(most, total([c == chip[k] for c in chip]))
    level_ref[0] = total([most > n for n in levels[:-1]])


def trace_kernel(
    slots,
    stock_ref, pick_in, shift_in, mirror_in, subcell_in, lens_in, filt_ref,
    deflect_ref, distort_ref,
    stock_t, bank, stage, own, beside, beside_out, far, far_out,
    pick_ref, shift_ref, mirror_ref, subcell_ref, lens_ref, mine, metas, edge32, edge_out, before, after, flank32, pairs, filt_v,
    hess, table,
    local_sem, small_sem, meta_send, meta_recv, push_send, push_recv, beside_send, beside_recv,
    far_send, far_recv, edge_send, edge_recv, *fields,
):
    held, blocks, ntiles = stock_ref.shape[:3]
    half = blocks // 2
    nrows, ncols = deflect_ref.shape[2:]
    cols = ntiles * TILE_C
    tiles = ncols // TILE_C
    planes = pick_ref.shape[0]
    peers, strips = lax.axis_size("real"), lax.axis_size("sky")
    chips = peers // 2
    me, strip = lax.axis_index("real"), lax.axis_index("sky")
    core, chip = lax.rem(me, 2), lax.div(me, 2)
    partner = me + 1 - 2 * core
    above = lax.rem(strip + strips - 1, strips)
    below = lax.rem(strip + 1, strips)
    outer = tiles * TILE_R
    head = outer + half * TILE_R
    span = fields[0].shape[1]
    bf = jnp.bfloat16
    f32 = jnp.float32
    low = max(0, planes - (chips - 1) * slots)
    high = min(slots, planes)

    def block_of(side, i):
        return side * (blocks - 1) + (1 - 2 * side) * i

    def remote(src, dst, send_sem, recv_sem, r, s):
        return pltpu.make_async_remote_copy(
            src_ref=src, dst_ref=dst, send_sem=send_sem, recv_sem=recv_sem,
            device_id=(r, s), device_id_type=MESH)

    small = [
        pltpu.make_async_copy(src, dst, small_sem.at[n])
        for n, (src, dst) in enumerate((
            (pick_in, pick_ref), (shift_in, shift_ref), (mirror_in, mirror_ref),
            (lens_in, lens_ref), (subcell_in, subcell_ref)))
    ]
    for copy in small:
        copy.start()
    stock_copy = pltpu.make_async_copy(stock_ref, stock_t, local_sem.at[0])
    stock_copy.start()
    barrier = pltpu.get_barrier_semaphore()
    for off in range(1, peers):
        pl.semaphore_signal(
            barrier, inc=1, device_id=(lax.rem(me + off, peers), strip), device_id_type=MESH)
    for s in (above, below):
        pl.semaphore_signal(barrier, inc=1, device_id=(me, s), device_id_type=MESH)
    bank_copies = [
        pltpu.make_async_copy(
            stock_ref.at[:, block_of(core, i)], bank.at[core, :, i], local_sem.at[1 + i])
        for i in range(half)
    ]
    filt_copy = pltpu.make_async_copy(filt_ref, filt_v, local_sem.at[1 + half])
    for copy in bank_copies + [filt_copy]:
        copy.start()

    for copy in small:
        copy.wait()
    for k in range(mine.shape[1]):
        mine[0, k] = 2 * shift_ref[0, k] + mirror_ref[0, k] if k < planes else 0
    for o in range(SUB):
        for m in range(NTAB):
            table[o, m] = f32(TABLE[o][m] / X_SCALE)
    edge32[...] = jnp.zeros_like(edge32)
    stage[...] = jnp.zeros_like(stage)

    pick = [pick_ref[k] for k in range(planes)]
    group = [lax.div(q, held) for q in pick]
    entry = [lax.rem(q, held) for q in pick]
    away = [lax.rem(lax.div(g, 2) - chip + chips, chips) for g in group]
    lane = [lax.rem(g, 2) for g in group]
    turn = [jnp.where(away[k] == 0, jnp.where(group[k] == me, 0, 1), lane[k]) for k in range(planes)]
    key = [(away[k] * 2 + turn[k]) * held + entry[k] for k in range(planes)]
    order = [total([key[n] < key[k] for n in range(planes)]) for k in range(planes)]
    plane_at = [last_hit([n == v for n in order], range(planes)) for v in range(planes)]
    n_own = total([group[k] == me for k in range(planes)])
    n_chip = total([away[k] == 0 for k in range(planes)])
    n_away = [total([away[k] == off for k in range(planes)]) for off in range(chips)]

    def chosen(inside, j):
        rank = [total([inside[n] & (pick[n] < pick[k]) for n in range(planes)]) for k in range(planes)]
        hits = [inside[k] & (rank[k] == j) for k in range(planes)]
        return [last_hit(hits, value) for value in (range(planes), lane, entry)]

    own_pick = [chosen([g == me for g in group], j) for j in range(held)]
    chip_pick = [chosen([a == 0 for a in away], j) for j in range(slots)]

    lane_in = lax.broadcasted_iota(jnp.int32, (2 * TILE_C, TILE_C), 0)
    lane_out = lax.broadcasted_iota(jnp.int32, (2 * TILE_C, TILE_C), 1)

    def cut(read, code, sides, out):
        turned = lax.rem(code, 2)
        shift = lax.div(code, 2)
        step = 1 - 2 * turned
        start = turned * (cols + EDGE - 1 - shift) + (1 - turned) * (shift + cols - EDGE)
        start = lax.rem(start, cols)
        base = lax.div(start, TILE_C)
        inner = start - base * TILE_C
        each_rows = (tiles + 2) * TILE_R
        for u in range(tiles + 2):
            at = lax.rem(base + step * u + ntiles, ntiles)
            for i in range(sides * half):
                row = i * each_rows + u * TILE_R
                stage[row:row + TILE_R, :] = read(i, at)
        near = lane_in == inner + step * lane_out
        far_ = lane_in - TILE_C == inner + step * (lane_out - TILE_C)
        choose = (near & (lane_in < TILE_C)) | (far_ & (lane_in >= TILE_C))
        choose = choose.astype(f32).astype(bf)
        n = sides * half * each_rows
        view = jnp.dot(
            jnp.concatenate([stage[0:n, :], stage[TILE_R:n + TILE_R, :]], axis=1), choose,
            preferred_element_type=f32)
        for x in range(sides):
            at = [(x * half + i) * each_rows for i in range(half)]
            rest = [view[a + outer:a + outer + TILE_R] for a in at]
            body_rows = [view[a:a + outer] for a in at]
            whole = jnp.concatenate(body_rows[:1] + rest + body_rows[1:], axis=0).astype(bf)
            out(x, whole)

    def code_of(r, k):
        return metas[r, 0, k]

    def own_read(e):
        def read(i, at):
            side, n = i // half, i % half
            return stock_t[e, block_of(side, n), at]
        return read

    def bank_read(c, e):
        def read(i, at):
            return bank[c, e, i, at]
        return read

    pl.semaphore_wait(barrier, peers + 1)

    def meta_copy(off):
        return remote(mine, metas.at[me], meta_send.at[off], meta_recv.at[off],
                      lax.rem(me + off, peers), strip)

    for off in range(1, peers):
        meta_copy(off).start()
    stock_copy.wait()
    push = [
        remote(stock_t.at[:, block_of(1 - core, i)], bank.at[core, :, i],
               push_send.at[i], push_recv.at[i], partner, strip)
        for i in range(half)
    ]
    for copy in push:
        copy.start()

    def keep(ref, *at):
        def out(x, whole):
            ref[(*at, x)] = whole
        return out

    for j in range(held):
        k, _, e = own_pick[j]
        cut(own_read(e), mine[0, k], 2, keep(own, j))

    for off in range(1, peers):
        meta_copy(off).wait()
    for copy in bank_copies:
        copy.wait()
    for copy in push:
        copy.wait()

    parts = (slice(0, head), slice(head, head + (half - 1) * outer))

    def far_copy(q, n, a, j):
        to = lax.rem(chip + n + 1, chips)
        return remote(
            far_out.at[n, a, j, parts[q]], far.at[chips - 2 - n, j, core, parts[q]],
            far_send.at[q, n, a, j], far_recv.at[q, chips - 2 - n, j, core],
            2 * to + a, strip)

    def far_arrived(q, n, j, side):
        return remote(
            far_out.at[n, 0, j, parts[q]], far.at[n, j, side, parts[q]],
            far_send.at[q, n, 0, j], far_recv.at[q, n, j, side], 2 * lax.rem(chip + n + 1, chips), strip)

    pieces = [(0, 0)]
    for j in range(1, slots):
        pieces += [(0, j), (1, j - 1)]
    pieces.append((1, slots - 1))
    sent = []

    def send_until(last):
        while last not in sent:
            q, j = pieces[len(sent)]
            sent.append((q, j))

            def go(n):
                for a in range(2):
                    far_copy(q, n, a, j).start()
            each(chips - 1, go)

    for j in range(slots):
        k, c, e = chip_pick[j]

        def make(n):
            to = lax.rem(chip + n + 1, chips)
            for a in range(2):
                def out(x, whole):
                    far_out[n, a, j] = whole
                cut(bank_read(c, e), code_of(2 * to + a, k), 1, out)
        each(chips - 1, make)
        if j < 2:
            send_until((0, j))
    send_until(pieces[-1])

    def beside_copy(j):
        return remote(beside_out.at[j], beside.at[j], beside_send.at[j], beside_recv.at[j], partner, strip)

    for j in range(held):
        k, _, e = own_pick[j]
        cut(own_read(e), code_of(partner, k), 2, keep(beside_out, j))
        beside_copy(j).start()

    def far_slots(v):
        if chips == 2:
            return [v - p for p in range(low, high + 1) if 0 <= v - p < slots]
        return list(range(min(v - low, slots - 1) + 1)) if v >= low else []

    arrived = set()

    def arrive(q, v):
        if v < high and "beside" not in arrived:
            arrived.add("beside")
            for j in range(held):
                beside_copy(j).wait_recv()
        for j in far_slots(v):
            if (q, j) not in arrived:
                arrived.add((q, j))

                def go(n):
                    for side in range(2):
                        far_arrived(q, n, j, side).wait_recv()
                each(chips - 1, go)

    def sources(v):
        found = []
        if v < high:
            if v < held:
                found.append((own.at[v], v < n_own))
            found += [(beside.at[j], (v - n_own == j) & (v < n_chip)) for j in range(held) if j <= v]
        gone = n_chip
        for n in range(chips - 1):
            for j in far_slots(v):
                found.append((far.at[n, j], (v - gone == j) & (j < n_away[n + 1])))
            gone = gone + n_away[n + 1]
        return found

    def selected(v, side, rows):
        got = None
        for ref, hit in sources(v):
            value = ref[side, rows, :]
            got = value if got is None else jnp.where(hit, value, got)
        return got

    def edge_copies(v):
        return [
            remote(edge_out.at[v, 0], after.at[v], edge_send.at[0, v], edge_recv.at[0, v], me, above),
            remote(edge_out.at[v, 1], before.at[v], edge_send.at[1, v], edge_recv.at[1, v], me, below),
        ]

    def lay(v, seg, side, first):
        left, right = slice(0, TILE_C), slice(TILE_C, 2 * TILE_C)
        pairs[v, seg, :, left] = selected(v, side, slice(first, first + outer))
        pairs[v, seg, 0:outer - TILE_R, right] = selected(v, side, slice(first + TILE_R, first + outer))

    def form_outer(v):
        arrive(0, v)
        for side in range(2):
            lay(v, side * half, side, 0)
            rest = selected(v, side, slice(outer, head))
            for i in range(half):
                pairs[v, side * half + i, outer - TILE_R:outer, TILE_C:2 * TILE_C] = (
                    rest[i * TILE_R:(i + 1) * TILE_R])
            shown = pairs[v, side * half, :, 0:TILE_C].astype(f32)
            ends = rest.astype(f32)[0:TILE_R]
            skip = side * (TILE_R - EDGE)
            for t in range(tiles):
                edge32[side, t * EDGE:(t + 1) * EDGE, :] = (
                    shown[t * TILE_R + skip:t * TILE_R + skip + EDGE])
            edge32[side, tiles * EDGE:(tiles + 1) * EDGE, :] = ends[skip:skip + EDGE]
            edge_out[v, side] = edge32[side].astype(bf)
        for copy in edge_copies(v):
            copy.start()

    def form_inner(v):
        arrive(1, v)
        for side in range(2):
            for i in range(1, half):
                lay(v, side * half + i, side, head + (i - 1) * outer)

    npairs = filt_ref.shape[1] // (2 * TILE_C)
    groups = tiles // span
    every = [(i, j) for j in range(tiles) for i in range(blocks)]

    def field_of(v, g):
        return fields[(v % 2) * groups + g]

    def filtered(lhs, c):
        return jnp.dot(
            jnp.concatenate([lhs, lhs], axis=1), filt_v[:, 2 * c * TILE_C:2 * (c + 1) * TILE_C],
            preferred_element_type=f32)

    def filter_own(v, g, c):
        field = field_of(v, g)
        rows = slice(g * span * TILE_R, (g + 1) * span * TILE_R)
        got = filtered(jnp.concatenate([pairs[v, seg, rows, :] for seg in range(blocks)], axis=0), c)
        for h in range(2):
            part = got[:, h * TILE_C:(h + 1) * TILE_C].reshape(blocks, span, TILE_R, TILE_C)
            for side in range(2):
                for i in range(half):
                    first = TILE_R * (1 + (blocks - 1 - i if side else i))
                    field[2 * c + h, :, first:first + TILE_R, :] = part[side * half + i]

    def filter_edges(vs, c):
        got = filtered(jnp.concatenate([pairs[v, blocks] for v in vs], axis=0), c)
        for h in range(2):
            part = got[:, h * TILE_C:(h + 1) * TILE_C].reshape(len(vs), groups, span, TILE_R, TILE_C)
            for n, v in enumerate(vs):
                for g in range(groups):
                    field_of(v, g)[2 * c + h, :, 0:TILE_R, :] = part[n, g]
                    field_of(v, g)[2 * c + h, :, TILE_R + nrows:2 * TILE_R + nrows, :] = part[n, g]

    def tile(v, i, j):
        field, jj = field_of(v, j // span), j % span
        lens = lens_ref[plane_at[v]]
        o = subcell_ref[i, j]
        oy = o // SUB
        fx = (o - oy * SUB) * 3
        wy = [table[oy, m] for m in range(NTAB)]
        y0, y1, y2 = wy[:4], wy[4:12], wy[12:20]

        def row(q, n):
            return field[fx + q, jj, pl.ds(TILE_R + i * TILE_R + n, TILE_R), :]
        plain = [row(0, n) for n in range(-3, 5)]
        slope = [row(1, n) for n in range(-3, 5)]
        curve = [row(2, n) for n in range(-1, 3)]
        gx = sum(y0[b] * slope[b + 2] for b in range(4))
        xx = sum(y0[b] * curve[b] for b in range(4))
        xy = sum(y1[b] * slope[b] for b in range(8))
        gy = sum(y1[b] * plain[b] for b in range(8))
        yy = sum(y2[b] * plain[b] for b in range(8))
        at = slice(j * TILE_C, (j + 1) * TILE_C)
        rs = slice(i * TILE_R, (i + 1) * TILE_R)
        for n, grad in enumerate((gx, gy)):
            old = deflect_ref[n, 0, rs, at] if v else 0.0
            deflect_ref[n, 0, rs, at] = old + lens * grad
        for n, h in enumerate((xx, xy, yy)):
            hess[v, n, j, rs, :] = lens * h

    def inner_blocks(v):
        for c in range(npairs):
            filter_own(v, 0, c)
        for g in range(groups):
            todo = [(i, j) for i, j in every if j // span == g and 0 < i < blocks - 1]
            count = -(-len(todo) // npairs)
            for c in range(npairs):
                if g + 1 < groups:
                    filter_own(v, g + 1, c)
                for i, j in todo[c * count:(c + 1) * count]:
                    tile(v, i, j)

    def bend(i, j):
        rs = slice(i * TILE_R, (i + 1) * TILE_R)
        at = slice(j * TILE_C, (j + 1) * TILE_C)
        shape = (TILE_R, TILE_C)
        zero, one = jnp.zeros(shape, f32), jnp.ones(shape, f32)
        a11, a12, a21, a22 = one, zero, zero, one
        for k in range(planes):
            xx, xy, yy = [hess[order[k], n, j, rs, :] for n in range(3)]
            a11, a12, a21, a22 = (
                a11 - (xx * a11 + xy * a21),
                a12 - (xx * a12 + xy * a22),
                a21 - (xy * a11 + yy * a21),
                a22 - (xy * a12 + yy * a22),
            )
        for n, a in enumerate((a11, a12, a21, a22)):
            distort_ref[n, 0, rs, at] = a

    def outer_blocks(vs, last):
        for v in vs:
            for copy in edge_copies(v):
                copy.wait_recv()
            up = before[v].astype(f32)
            down = after[v].astype(f32)
            for t in range(tiles + 1):
                flank32[t, EDGE:2 * EDGE, :] = up[t * EDGE:(t + 1) * EDGE]
                flank32[t, 0:EDGE, :] = down[t * EDGE:(t + 1) * EDGE]
            for side in range(2):
                pairs[v, blocks, :, side * TILE_C:(side + 1) * TILE_C] = (
                    flank32[side:tiles + side].reshape(outer, TILE_C).astype(bf))
        inner = [(i, j) for i, j in every if 0 < i < blocks - 1] if last else []
        count = -(-len(inner) // npairs)
        for c in range(npairs):
            filter_edges(vs, c)
            for i, j in inner[c * count:(c + 1) * count]:
                bend(i, j)
        for i, j in every:
            if i in (0, blocks - 1):
                for v in vs:
                    tile(v, i, j)
                if last:
                    bend(i, j)

    filt_copy.wait()
    for v in range(low):
        form_outer(v)
    for v in range(low):
        form_inner(v)
        inner_blocks(v)
    rest = list(range(low, planes))
    for v in rest[:2]:
        form_outer(v)
    behind = list(range(low))
    for n, v in enumerate(rest):
        if len(behind) >= 2:
            outer_blocks(behind[:2], False)
            behind = behind[2:]
        form_inner(v)
        inner_blocks(v)
        behind.append(v)
        if n + 2 < len(rest):
            form_outer(rest[n + 2])
    while behind:
        outer_blocks(behind[:2], len(behind) <= 2)
        behind = behind[2:]

    for j in range(held):
        beside_copy(j).wait_send()
    for j in range(slots):
        def done(n):
            for a in range(2):
                for q in range(2):
                    far_copy(q, n, a, j).wait_send()
        each(chips - 1, done)
    for v in range(planes):
        for copy in edge_copies(v):
            copy.wait_send()


def body(potential_stock, plane_pick, col_shift, mirror, subcell, lens_weight):
    held, rows, cols = potential_stock.shape
    peers = lax.axis_size("real")
    planes = plane_pick.shape[0]
    ncols = subcell.shape[1] * TILE_C
    nrows = subcell.shape[0] * TILE_R
    tiles = ncols // TILE_C
    blocks, half = rows // TILE_R, rows // (2 * TILE_R)
    chips = peers // 2
    ntiles = cols // TILE_C
    stock = potential_stock.reshape(held, blocks, TILE_R, ntiles, TILE_C).transpose(0, 1, 3, 2, 4)
    vm = pl.BlockSpec(memory_space=pltpu.VMEM)
    anyw = pl.BlockSpec(memory_space=pl.ANY)
    bf, f32 = jnp.bfloat16, jnp.float32
    dma = pltpu.SemaphoreType.DMA
    win = half * TILE_R * (tiles + 1)
    erows = -(-((tiles + 1) * EDGE) // 16) * 16
    srows = 2 * half * (tiles + 2) * TILE_R + 16
    span = next(d for d in (8, 4, 2, 1) if tiles % d == 0)
    filt = jnp.asarray(column_filters())
    meta = max(8, planes)
    def traced(slots, *arrays):
        return pl.pallas_call(
            functools.partial(trace_kernel, slots),
            out_shape=(
                pltpu.VMEM((2, 1, nrows, ncols), f32),
                pltpu.VMEM((4, 1, nrows, ncols), f32),
            ),
            in_specs=[anyw] * 7,
            out_specs=(vm, vm),
            scratch_shapes=[
                pltpu.VMEM(stock.shape, bf),
                pltpu.VMEM((2, held, half, ntiles, TILE_R, TILE_C), bf),
                pltpu.VMEM((srows, TILE_C), bf),
                pltpu.VMEM((held, 2, win, TILE_C), bf),
                pltpu.VMEM((held, 2, win, TILE_C), bf),
                pltpu.VMEM((held, 2, win, TILE_C), bf),
                pltpu.VMEM((chips - 1, slots, 2, win, TILE_C), bf),
                pltpu.VMEM((chips - 1, 2, slots, win, TILE_C), bf),
                pltpu.SMEM(plane_pick.shape, jnp.int32),
                pltpu.SMEM(col_shift.shape, jnp.int32),
                pltpu.SMEM(mirror.shape, jnp.int32),
                pltpu.SMEM(subcell.shape, jnp.int32),
                pltpu.SMEM(lens_weight.shape, f32),
                pltpu.SMEM((1, meta), jnp.int32),
                pltpu.SMEM((peers, 1, meta), jnp.int32),
                pltpu.VMEM((2, erows, TILE_C), f32),
                pltpu.VMEM((planes, 2, erows, TILE_C), bf),
                pltpu.VMEM((planes, erows, TILE_C), bf),
                pltpu.VMEM((planes, erows, TILE_C), bf),
                pltpu.VMEM((tiles + 1, TILE_R, TILE_C), f32),
                pltpu.VMEM((planes, blocks + 1, tiles * TILE_R, 2 * TILE_C), bf),
                pltpu.VMEM(filt.shape, bf),
                pltpu.VMEM((planes, 3, tiles, nrows, TILE_C), f32),
                pltpu.SMEM((SUB, NTAB), f32),
                dma((2 + half,)), dma((5,)),
                dma((peers,)), dma((peers,)),
                dma((half,)), dma((half,)),
                dma((held,)), dma((held,)),
                dma((2, chips - 1, 2, slots)), dma((2, chips - 1, slots, 2)),
                dma((2, planes)), dma((2, planes)),
            ] + [
                pltpu.VMEM((SUB * 3, span, nrows + 2 * TILE_R, TILE_C), f32)
            ] * (2 * tiles // span),
            compiler_params=pltpu.CompilerParams(
                collective_id=levels.index(slots), has_side_effects=True, vmem_limit_bytes=61 * 1024 * 1024),
            name="trace_%d" % slots,
        )(*arrays)

    least, most = -(-planes // chips), min(planes, 2 * held)
    levels = sorted({least, min(least + 1, most), most})
    arrays = (stock, plane_pick, col_shift, mirror, subcell, lens_weight, filt)
    if len(levels) == 1:
        return traced(most, *arrays)
    sm = pl.BlockSpec(memory_space=pltpu.SMEM)
    level = pl.pallas_call(
        functools.partial(level_kernel, 2 * held, levels),
        out_shape=jax.ShapeDtypeStruct((1,), jnp.int32),
        in_specs=[sm], out_specs=sm, name="level",
    )(plane_pick)
    return lax.switch(level[0], [functools.partial(traced, n) for n in levels], *arrays)


def solution(mesh):
    return jax.shard_map(
        body,
        mesh=mesh,
        in_specs=(
            P("real", "sky", None),
            P(),
            P("real", None),
            P("real", None),
            P("sky", None),
            P(),
        ),
        out_specs=(P(None, "real", "sky", None), P(None, "real", "sky", None)),
        check_vma=False,
    )
```

```python
import functools

import jax
import jax.numpy as jnp
import numpy as np
from jax import lax
from jax.experimental import pallas as pl
from jax.experimental.pallas import tpu as pltpu
from jax.sharding import PartitionSpec as P

SUB = 4
TILE_R = 8
TILE_C = 128
EDGE = 4
MESH = pl.DeviceIdType.MESH

first_coef = (1.0 / 12.0, -8.0 / 12.0, 0.0, 8.0 / 12.0, -1.0 / 12.0)
second_coef = (-1.0 / 12.0, 16.0 / 12.0, -30.0 / 12.0, 16.0 / 12.0, -1.0 / 12.0)


def cubic(t):
    return (
        (-(t**3) + 2 * t**2 - t) / 2,
        (3 * t**3 - 5 * t**2 + 2) / 2,
        (-3 * t**3 + 4 * t**2 + t) / 2,
        (t**3 - t**2) / 2,
    )


def convolved(taps, coef):
    out = [0.0] * 8
    for a, w in enumerate(taps):
        for q, c in enumerate(coef):
            out[a + q] += w * c
    return out


def filter_table():
    rows = []
    for o in range(SUB):
        taps = cubic((o + 0.5) / SUB)
        rows.append(list(taps) + convolved(taps, first_coef) + convolved(taps, second_coef))
    return rows


TABLE = filter_table()
NTAB = 20
X_SCALE = 12288.0


def column_filters():
    full = np.zeros((2 * TILE_C, SUB, 3, TILE_C))
    out = np.arange(TILE_C)
    for o, row in enumerate(TABLE):
        for m in range(4):
            full[out + 3 + m, o, 0, out] = row[m] * X_SCALE
        for m in range(8):
            full[out + 1 + m, o, 1, out] = row[4 + m] * X_SCALE
            full[out + 1 + m, o, 2, out] = row[12 + m] * X_SCALE
    full = np.rint(full.reshape(2 * TILE_C, SUB * 3 * TILE_C)).astype(np.float32)
    high = full.astype(jnp.bfloat16)
    low = (full - high.astype(np.float32)).astype(jnp.bfloat16)
    return np.concatenate([high, low], axis=0)


def each(count, fn):
    if count == 1:
        fn(0)
    else:
        lax.fori_loop(0, count, lambda n, carry: (fn(n), carry)[1], 0)


def total(flags):
    return sum(jnp.where(flag, 1, 0) for flag in flags)


def last_hit(hits, values):
    found = jnp.int32(0)
    for hit, value in zip(hits, values):
        found = jnp.where(hit, value, found)
    return found


def level_kernel(per_chip, levels, pick_ref, level_ref):
    planes = pick_ref.shape[0]
    chip = [lax.div(pick_ref[k], per_chip) for k in range(planes)]
    most = jnp.int32(0)
    for k in range(planes):
        most = jnp.maximum(most, total([c == chip[k] for c in chip]))
    level_ref[0] = total([most > n for n in levels[:-1]])


def trace_kernel(
    slots,
    stock_ref, pick_in, shift_in, mirror_in, subcell_in, lens_in, filt_ref,
    deflect_ref, distort_ref,
    stock_t, bank, stage, own, beside, beside_out, far, far_out,
    pick_ref, shift_ref, mirror_ref, subcell_ref, lens_ref, mine, metas, edge32, edge_out, before, after, flank32, pairs, filt_v,
    hess, table,
    local_sem, small_sem, meta_send, meta_recv, push_send, push_recv, beside_send, beside_recv,
    far_send, far_recv, edge_send, edge_recv, *fields,
):
    held, blocks, ntiles = stock_ref.shape[:3]
    half = blocks // 2
    nrows, ncols = deflect_ref.shape[2:]
    cols = ntiles * TILE_C
    tiles = ncols // TILE_C
    planes = pick_ref.shape[0]
    peers, strips = lax.axis_size("real"), lax.axis_size("sky")
    chips = peers // 2
    me, strip = lax.axis_index("real"), lax.axis_index("sky")
    core, chip = lax.rem(me, 2), lax.div(me, 2)
    partner = me + 1 - 2 * core
    above = lax.rem(strip + strips - 1, strips)
    below = lax.rem(strip + 1, strips)
    outer = tiles * TILE_R
    head = outer + half * TILE_R
    span = fields[0].shape[1]
    bf = jnp.bfloat16
    f32 = jnp.float32
    low = max(0, planes - (chips - 1) * slots)
    high = min(slots, planes)

    def block_of(side, i):
        return side * (blocks - 1) + (1 - 2 * side) * i

    def remote(src, dst, send_sem, recv_sem, r, s):
        return pltpu.make_async_remote_copy(
            src_ref=src, dst_ref=dst, send_sem=send_sem, recv_sem=recv_sem,
            device_id=(r, s), device_id_type=MESH)

    small = [
        pltpu.make_async_copy(src, dst, small_sem.at[n])
        for n, (src, dst) in enumerate((
            (pick_in, pick_ref), (shift_in, shift_ref), (mirror_in, mirror_ref),
            (lens_in, lens_ref), (subcell_in, subcell_ref)))
    ]
    for copy in small:
        copy.start()
    stock_copy = pltpu.make_async_copy(stock_ref, stock_t, local_sem.at[0])
    stock_copy.start()
    barrier = pltpu.get_barrier_semaphore()
    for off in range(1, peers):
        pl.semaphore_signal(
            barrier, inc=1, device_id=(lax.rem(me + off, peers), strip), device_id_type=MESH)
    for s in (above, below):
        pl.semaphore_signal(barrier, inc=1, device_id=(me, s), device_id_type=MESH)
    bank_copies = [
        pltpu.make_async_copy(
            stock_ref.at[:, block_of(core, i)], bank.at[core, :, i], local_sem.at[1 + i])
        for i in range(half)
    ]
    filt_copy = pltpu.make_async_copy(filt_ref, filt_v, local_sem.at[1 + half])
    for copy in bank_copies + [filt_copy]:
        copy.start()

    for copy in small:
        copy.wait()
    for k in range(mine.shape[1]):
        mine[0, k] = 2 * shift_ref[0, k] + mirror_ref[0, k] if k < planes else 0
    for o in range(SUB):
        for m in range(NTAB):
            table[o, m] = f32(TABLE[o][m] / X_SCALE)
    edge32[...] = jnp.zeros_like(edge32)
    stage[...] = jnp.zeros_like(stage)

    pick = [pick_ref[k] for k in range(planes)]
    group = [lax.div(q, held) for q in pick]
    entry = [lax.rem(q, held) for q in pick]
    away = [lax.rem(lax.div(g, 2) - chip + chips, chips) for g in group]
    lane = [lax.rem(g, 2) for g in group]
    turn = [jnp.where(away[k] == 0, jnp.where(group[k] == me, 0, 1), lane[k]) for k in range(planes)]
    key = [(away[k] * 2 + turn[k]) * held + entry[k] for k in range(planes)]
    order = [total([key[n] < key[k] for n in range(planes)]) for k in range(planes)]
    plane_at = [last_hit([n == v for n in order], range(planes)) for v in range(planes)]
    n_own = total([group[k] == me for k in range(planes)])
    n_chip = total([away[k] == 0 for k in range(planes)])
    n_away = [total([away[k] == off for k in range(planes)]) for off in range(chips)]

    def chosen(inside, j):
        rank = [total([inside[n] & (pick[n] < pick[k]) for n in range(planes)]) for k in range(planes)]
        hits = [inside[k] & (rank[k] == j) for k in range(planes)]
        return [last_hit(hits, value) for value in (range(planes), lane, entry)]

    own_pick = [chosen([g == me for g in group], j) for j in range(held)]
    chip_pick = [chosen([a == 0 for a in away], j) for j in range(slots)]

    lane_in = lax.broadcasted_iota(jnp.int32, (2 * TILE_C, TILE_C), 0)
    lane_out = lax.broadcasted_iota(jnp.int32, (2 * TILE_C, TILE_C), 1)

    def cut(read, code, sides, out):
        turned = lax.rem(code, 2)
        shift = lax.div(code, 2)
        step = 1 - 2 * turned
        start = turned * (cols + EDGE - 1 - shift) + (1 - turned) * (shift + cols - EDGE)
        start = lax.rem(start, cols)
        base = lax.div(start, TILE_C)
        inner = start - base * TILE_C
        each_rows = (tiles + 2) * TILE_R
        for u in range(tiles + 2):
            at = lax.rem(base + step * u + ntiles, ntiles)
            for i in range(sides * half):
                row = i * each_rows + u * TILE_R
                stage[row:row + TILE_R, :] = read(i, at)
        near = lane_in == inner + step * lane_out
        far_ = lane_in - TILE_C == inner + step * (lane_out - TILE_C)
        choose = (near & (lane_in < TILE_C)) | (far_ & (lane_in >= TILE_C))
        choose = choose.astype(f32).astype(bf)
        n = sides * half * each_rows
        view = jnp.dot(
            jnp.concatenate([stage[0:n, :], stage[TILE_R:n + TILE_R, :]], axis=1), choose,
            preferred_element_type=f32)
        for x in range(sides):
            at = [(x * half + i) * each_rows for i in range(half)]
            rest = [view[a + outer:a + outer + TILE_R] for a in at]
            body_rows = [view[a:a + outer] for a in at]
            whole = jnp.concatenate(body_rows[:1] + rest + body_rows[1:], axis=0).astype(bf)
            out(x, whole)

    def code_of(r, k):
        return metas[r, 0, k]

    def own_read(e):
        def read(i, at):
            side, n = i // half, i % half
            return stock_t[e, block_of(side, n), at]
        return read

    def bank_read(c, e):
        def read(i, at):
            return bank[c, e, i, at]
        return read

    pl.semaphore_wait(barrier, peers + 1)

    def meta_copy(off):
        return remote(mine, metas.at[me], meta_send.at[off], meta_recv.at[off],
                      lax.rem(me + off, peers), strip)

    for off in range(1, peers):
        meta_copy(off).start()
    stock_copy.wait()
    push = [
        remote(stock_t.at[:, block_of(1 - core, i)], bank.at[core, :, i],
               push_send.at[i], push_recv.at[i], partner, strip)
        for i in range(half)
    ]
    for copy in push:
        copy.start()

    def keep(ref, *at):
        def out(x, whole):
            ref[(*at, x)] = whole
        return out

    for j in range(held):
        k, _, e = own_pick[j]
        cut(own_read(e), mine[0, k], 2, keep(own, j))

    for off in range(1, peers):
        meta_copy(off).wait()
    for copy in bank_copies:
        copy.wait()
    for copy in push:
        copy.wait()

    parts = (slice(0, head), slice(head, head + (half - 1) * outer))

    def far_copy(q, n, a, j):
        to = lax.rem(chip + n + 1, chips)
        return remote(
            far_out.at[n, a, j, parts[q]], far.at[chips - 2 - n, j, core, parts[q]],
            far_send.at[q, n, a, j], far_recv.at[q, chips - 2 - n, j, core],
            2 * to + a, strip)

    def far_arrived(q, n, j, side):
        return remote(
            far_out.at[n, 0, j, parts[q]], far.at[n, j, side, parts[q]],
            far_send.at[q, n, 0, j], far_recv.at[q, n, j, side], 2 * lax.rem(chip + n + 1, chips), strip)

    pieces = [(0, 0)]
    for j in range(1, slots):
        pieces += [(0, j), (1, j - 1)]
    pieces.append((1, slots - 1))
    sent = []

    def send_until(last):
        while last not in sent:
            q, j = pieces[len(sent)]
            sent.append((q, j))

            def go(n):
                for a in range(2):
                    far_copy(q, n, a, j).start()
            each(chips - 1, go)

    for j in range(slots):
        k, c, e = chip_pick[j]

        def make(n):
            to = lax.rem(chip + n + 1, chips)
            for a in range(2):
                def out(x, whole):
                    far_out[n, a, j] = whole
                cut(bank_read(c, e), code_of(2 * to + a, k), 1, out)
        each(chips - 1, make)
        if j < 2:
            send_until((0, j))
    send_until(pieces[-1])

    def beside_copy(j):
        return remote(beside_out.at[j], beside.at[j], beside_send.at[j], beside_recv.at[j], partner, strip)

    for j in range(held):
        k, _, e = own_pick[j]
        cut(own_read(e), code_of(partner, k), 2, keep(beside_out, j))
        beside_copy(j).start()

    def far_slots(v):
        if chips == 2:
            return [v - p for p in range(low, high + 1) if 0 <= v - p < slots]
        return list(range(min(v - low, slots - 1) + 1)) if v >= low else []

    arrived = set()

    def arrive(q, v):
        if v < high and "beside" not in arrived:
            arrived.add("beside")
            for j in range(held):
                beside_copy(j).wait_recv()
        for j in far_slots(v):
            if (q, j) not in arrived:
                arrived.add((q, j))

                def go(n):
                    for side in range(2):
                        far_arrived(q, n, j, side).wait_recv()
                each(chips - 1, go)

    def sources(v):
        found = []
        if v < high:
            if v < held:
                found.append((own.at[v], v < n_own))
            found += [(beside.at[j], (v - n_own == j) & (v < n_chip)) for j in range(held) if j <= v]
        gone = n_chip
        for n in range(chips - 1):
            for j in far_slots(v):
                found.append((far.at[n, j], (v - gone == j) & (j < n_away[n + 1])))
            gone = gone + n_away[n + 1]
        return found

    def selected(v, side, rows):
        got = None
        for ref, hit in sources(v):
            value = ref[side, rows, :]
            got = value if got is None else jnp.where(hit, value, got)
        return got

    def edge_copies(v):
        return [
            remote(edge_out.at[v, 0], after.at[v], edge_send.at[0, v], edge_recv.at[0, v], me, above),
            remote(edge_out.at[v, 1], before.at[v], edge_send.at[1, v], edge_recv.at[1, v], me, below),
        ]

    def lay(v, seg, side, first):
        left, right = slice(0, TILE_C), slice(TILE_C, 2 * TILE_C)
        pairs[v, seg, :, left] = selected(v, side, slice(first, first + outer))
        pairs[v, seg, 0:outer - TILE_R, right] = selected(v, side, slice(first + TILE_R, first + outer))

    def form_outer(v):
        arrive(0, v)
        for side in range(2):
            lay(v, side * half, side, 0)
            rest = selected(v, side, slice(outer, head))
            for i in range(half):
                pairs[v, side * half + i, outer - TILE_R:outer, TILE_C:2 * TILE_C] = (
                    rest[i * TILE_R:(i + 1) * TILE_R])
            shown = pairs[v, side * half, :, 0:TILE_C].astype(f32)
            ends = rest.astype(f32)[0:TILE_R]
            skip = side * (TILE_R - EDGE)
            for t in range(tiles):
                edge32[side, t * EDGE:(t + 1) * EDGE, :] = (
                    shown[t * TILE_R + skip:t * TILE_R + skip + EDGE])
            edge32[side, tiles * EDGE:(tiles + 1) * EDGE, :] = ends[skip:skip + EDGE]
            edge_out[v, side] = edge32[side].astype(bf)
        for copy in edge_copies(v):
            copy.start()

    def form_inner(v):
        arrive(1, v)
        for side in range(2):
            for i in range(1, half):
                lay(v, side * half + i, side, head + (i - 1) * outer)

    npairs = filt_ref.shape[1] // (2 * TILE_C)
    groups = tiles // span
    every = [(i, j) for j in range(tiles) for i in range(blocks)]

    def field_of(v, g):
        return fields[(v % 2) * groups + g]

    def filtered(lhs, c):
        return jnp.dot(
            jnp.concatenate([lhs, lhs], axis=1), filt_v[:, 2 * c * TILE_C:2 * (c + 1) * TILE_C],
            preferred_element_type=f32)

    def filter_own(v, g, c):
        field = field_of(v, g)
        rows = slice(g * span * TILE_R, (g + 1) * span * TILE_R)
        got = filtered(jnp.concatenate([pairs[v, seg, rows, :] for seg in range(blocks)], axis=0), c)
        for h in range(2):
            part = got[:, h * TILE_C:(h + 1) * TILE_C].reshape(blocks, span, TILE_R, TILE_C)
            for side in range(2):
                for i in range(half):
                    first = TILE_R * (1 + (blocks - 1 - i if side else i))
                    field[2 * c + h, :, first:first + TILE_R, :] = part[side * half + i]

    def filter_edges(vs, c):
        got = filtered(jnp.concatenate([pairs[v, blocks] for v in vs], axis=0), c)
        for h in range(2):
            part = got[:, h * TILE_C:(h + 1) * TILE_C].reshape(len(vs), groups, span, TILE_R, TILE_C)
            for n, v in enumerate(vs):
                for g in range(groups):
                    field_of(v, g)[2 * c + h, :, 0:TILE_R, :] = part[n, g]
                    field_of(v, g)[2 * c + h, :, TILE_R + nrows:2 * TILE_R + nrows, :] = part[n, g]

    def tile(v, i, j):
        field, jj = field_of(v, j // span), j % span
        lens = lens_ref[plane_at[v]]
        o = subcell_ref[i, j]
        oy = o // SUB
        fx = (o - oy * SUB) * 3
        wy = [table[oy, m] for m in range(NTAB)]
        y0, y1, y2 = wy[:4], wy[4:12], wy[12:20]

        def row(q, n):
            return field[fx + q, jj, pl.ds(TILE_R + i * TILE_R + n, TILE_R), :]
        plain = [row(0, n) for n in range(-3, 5)]
        slope = [row(1, n) for n in range(-3, 5)]
        curve = [row(2, n) for n in range(-1, 3)]
        gx = sum(y0[b] * slope[b + 2] for b in range(4))
        xx = sum(y0[b] * curve[b] for b in range(4))
        xy = sum(y1[b] * slope[b] for b in range(8))
        gy = sum(y1[b] * plain[b] for b in range(8))
        yy = sum(y2[b] * plain[b] for b in range(8))
        at = slice(j * TILE_C, (j + 1) * TILE_C)
        rs = slice(i * TILE_R, (i + 1) * TILE_R)
        for n, grad in enumerate((gx, gy)):
            old = deflect_ref[n, 0, rs, at] if v else 0.0
            deflect_ref[n, 0, rs, at] = old + lens * grad
        for n, h in enumerate((xx, xy, yy)):
            hess[v, n, j, rs, :] = lens * h

    def inner_blocks(v):
        for c in range(npairs):
            filter_own(v, 0, c)
        for g in range(groups):
            todo = [(i, j) for i, j in every if j // span == g and 0 < i < blocks - 1]
            count = -(-len(todo) // npairs)
            for c in range(npairs):
                if g + 1 < groups:
                    filter_own(v, g + 1, c)
                for i, j in todo[c * count:(c + 1) * count]:
                    tile(v, i, j)

    def bend(i, j):
        rs = slice(i * TILE_R, (i + 1) * TILE_R)
        at = slice(j * TILE_C, (j + 1) * TILE_C)
        shape = (TILE_R, TILE_C)
        zero, one = jnp.zeros(shape, f32), jnp.ones(shape, f32)
        a11, a12, a21, a22 = one, zero, zero, one
        for k in range(planes):
            xx, xy, yy = [hess[order[k], n, j, rs, :] for n in range(3)]
            a11, a12, a21, a22 = (
                a11 - (xx * a11 + xy * a21),
                a12 - (xx * a12 + xy * a22),
                a21 - (xy * a11 + yy * a21),
                a22 - (xy * a12 + yy * a22),
            )
        for n, a in enumerate((a11, a12, a21, a22)):
            distort_ref[n, 0, rs, at] = a

    def outer_blocks(vs, last):
        for v in vs:
            for copy in edge_copies(v):
                copy.wait_recv()
            up = before[v].astype(f32)
            down = after[v].astype(f32)
            for t in range(tiles + 1):
                flank32[t, EDGE:2 * EDGE, :] = up[t * EDGE:(t + 1) * EDGE]
                flank32[t, 0:EDGE, :] = down[t * EDGE:(t + 1) * EDGE]
            for side in range(2):
                pairs[v, blocks, :, side * TILE_C:(side + 1) * TILE_C] = (
                    flank32[side:tiles + side].reshape(outer, TILE_C).astype(bf))
        inner = [(i, j) for i, j in every if 0 < i < blocks - 1] if last else []
        count = -(-len(inner) // npairs)
        for c in range(npairs):
            filter_edges(vs, c)
            for i, j in inner[c * count:(c + 1) * count]:
                bend(i, j)
        for i, j in every:
            if i in (0, blocks - 1):
                for v in vs:
                    tile(v, i, j)
                if last:
                    bend(i, j)

    filt_copy.wait()
    for v in range(low):
        form_outer(v)
    for v in range(low):
        form_inner(v)
        inner_blocks(v)
    rest = list(range(low, planes))
    for v in rest[:2]:
        form_outer(v)
    behind = list(range(low))
    for n, v in enumerate(rest):
        if len(behind) >= 2:
            outer_blocks(behind[:2], False)
            behind = behind[2:]
        form_inner(v)
        inner_blocks(v)
        behind.append(v)
        if n + 2 < len(rest):
            form_outer(rest[n + 2])
    while behind:
        outer_blocks(behind[:2], len(behind) <= 2)
        behind = behind[2:]

    for j in range(held):
        beside_copy(j).wait_send()
    for j in range(slots):
        def done(n):
            for a in range(2):
                for q in range(2):
                    far_copy(q, n, a, j).wait_send()
        each(chips - 1, done)
    for v in range(planes):
        for copy in edge_copies(v):
            copy.wait_send()


def body(potential_stock, plane_pick, col_shift, mirror, subcell, lens_weight):
    held, rows, cols = potential_stock.shape
    peers = lax.axis_size("real")
    planes = plane_pick.shape[0]
    ncols = subcell.shape[1] * TILE_C
    nrows = subcell.shape[0] * TILE_R
    tiles = ncols // TILE_C
    blocks, half = rows // TILE_R, rows // (2 * TILE_R)
    chips = peers // 2
    ntiles = cols // TILE_C
    stock = potential_stock.reshape(held, blocks, TILE_R, ntiles, TILE_C).transpose(0, 1, 3, 2, 4)
    vm = pl.BlockSpec(memory_space=pltpu.VMEM)
    anyw = pl.BlockSpec(memory_space=pl.ANY)
    bf, f32 = jnp.bfloat16, jnp.float32
    dma = pltpu.SemaphoreType.DMA
    win = half * TILE_R * (tiles + 1)
    erows = -(-((tiles + 1) * EDGE) // 16) * 16
    srows = 2 * half * (tiles + 2) * TILE_R + 16
    span = next(d for d in (4, 2, 1) if tiles % d == 0)
    filt = jnp.asarray(column_filters())
    meta = max(8, planes)
    def traced(slots, *arrays):
        return pl.pallas_call(
            functools.partial(trace_kernel, slots),
            out_shape=(
                pltpu.VMEM((2, 1, nrows, ncols), f32),
                pltpu.VMEM((4, 1, nrows, ncols), f32),
            ),
            in_specs=[anyw] * 7,
            out_specs=(vm, vm),
            scratch_shapes=[
                pltpu.VMEM(stock.shape, bf),
                pltpu.VMEM((2, held, half, ntiles, TILE_R, TILE_C), bf),
                pltpu.VMEM((srows, TILE_C), bf),
                pltpu.VMEM((held, 2, win, TILE_C), bf),
                pltpu.VMEM((held, 2, win, TILE_C), bf),
                pltpu.VMEM((held, 2, win, TILE_C), bf),
                pltpu.VMEM((chips - 1, slots, 2, win, TILE_C), bf),
                pltpu.VMEM((chips - 1, 2, slots, win, TILE_C), bf),
                pltpu.SMEM(plane_pick.shape, jnp.int32),
                pltpu.SMEM(col_shift.shape, jnp.int32),
                pltpu.SMEM(mirror.shape, jnp.int32),
                pltpu.SMEM(subcell.shape, jnp.int32),
                pltpu.SMEM(lens_weight.shape, f32),
                pltpu.SMEM((1, meta), jnp.int32),
                pltpu.SMEM((peers, 1, meta), jnp.int32),
                pltpu.VMEM((2, erows, TILE_C), f32),
                pltpu.VMEM((planes, 2, erows, TILE_C), bf),
                pltpu.VMEM((planes, erows, TILE_C), bf),
                pltpu.VMEM((planes, erows, TILE_C), bf),
                pltpu.VMEM((tiles + 1, TILE_R, TILE_C), f32),
                pltpu.VMEM((planes, blocks + 1, tiles * TILE_R, 2 * TILE_C), bf),
                pltpu.VMEM(filt.shape, bf),
                pltpu.VMEM((planes, 3, tiles, nrows, TILE_C), f32),
                pltpu.SMEM((SUB, NTAB), f32),
                dma((2 + half,)), dma((5,)),
                dma((peers,)), dma((peers,)),
                dma((half,)), dma((half,)),
                dma((held,)), dma((held,)),
                dma((2, chips - 1, 2, slots)), dma((2, chips - 1, slots, 2)),
                dma((2, planes)), dma((2, planes)),
            ] + [
                pltpu.VMEM((SUB * 3, span, nrows + 2 * TILE_R, TILE_C), f32)
            ] * (2 * tiles // span),
            compiler_params=pltpu.CompilerParams(
                collective_id=levels.index(slots), has_side_effects=True, vmem_limit_bytes=61 * 1024 * 1024),
            name="trace_%d" % slots,
        )(*arrays)

    least, most = -(-planes // chips), min(planes, 2 * held)
    levels = sorted({least, min(least + 1, most), most})
    arrays = (stock, plane_pick, col_shift, mirror, subcell, lens_weight, filt)
    if len(levels) == 1:
        return traced(most, *arrays)
    sm = pl.BlockSpec(memory_space=pltpu.SMEM)
    level = pl.pallas_call(
        functools.partial(level_kernel, 2 * held, levels),
        out_shape=jax.ShapeDtypeStruct((1,), jnp.int32),
        in_specs=[sm], out_specs=sm, name="level",
    )(plane_pick)
    return lax.switch(level[0], [functools.partial(traced, n) for n in levels], *arrays)


def solution(mesh):
    return jax.shard_map(
        body,
        mesh=mesh,
        in_specs=(
            P("real", "sky", None),
            P(),
            P("real", None),
            P("real", None),
            P("sky", None),
            P(),
        ),
        out_specs=(P(None, "real", "sky", None), P(None, "real", "sky", None)),
        check_vma=False,
    )
```
